512 devices in a mesh: dp: 64 (over x, z_lo, y), tensor: 4 (over z_hi), section: 2 (over core).
Axes of the slice: x: 4, y: 8, z: 8 (z_hi: 4, z_lo: 2; z = z_hi * 2 + z_lo), core: 2. Of those that a mesh axis runs over, the one named last changes fastest.
Arguments:
- train_act: bfloat16 [2, 16384, 8192], P('section', ('dp', 'tensor')), may hold values from -6 to 6
- train_grad: bfloat16 [2, 16384, 28672], P('section', 'dp', 'tensor'), may hold values from -6 to 6
- val_act: bfloat16 [2, 256, 8192], P('section', 'dp'), may hold values from -6 to 6
- val_grad: bfloat16 [2, 256, 28672], P('section', 'dp', 'tensor'), may hold values from -6 to 6
Outputs:
- scores: float32 [16384], P(('dp', 'tensor', 'section'))
The draws below stay inside these ranges and needn't reach their ends.
All inputs are finite; a program needn't handle non-finite values.
Results may differ from the reference program's by a relative error of at most 0.0003.
Values may be sent and summed in bfloat16 or wider, within the bound.
No kernel may reach another device: no remote copies, remote signals or barrier semaphores. Data moves between devices by JAX's collectives and lax.ppermute only.
A program may use at most 64 MiB of HBM per device.

```python
import math
import jax
import jax.numpy as jnp
from jax import lax

D = 8192
FF = 28672
LAYERS = 2
TOKENS = 16384
VTOK = 256


def block_levels(key, extent, cuts, least, top_value):
    loudness = 1.0
    for position, shards_of in cuts:
        steps = jax.random.uniform(jax.random.fold_in(jax.random.fold_in(key, 6), position), (shards_of,), jnp.float32, least / len(cuts), top_value / len(cuts))
        loudness = loudness * jnp.repeat(jnp.exp(steps), extent[position] // shards_of).reshape((-1,) + (1,) * (len(extent) - 1 - position))
    return loudness


def gaussian(rng, dims, deviation, most, shards=(), kind=jnp.bfloat16):
    array = jax.random.normal(rng, dims, jnp.float32) * deviation
    if len(shards) > 0:
        array = block_levels(rng, dims, shards, -0.22, 0.18) * array
    return jnp.clip(array, min=-most, max=most).astype(kind)


def setup_inputs(seed: int = 0) -> dict:
    seeds = jax.random.split(jax.random.key(seed), 5)
    return {
        "train_act": gaussian(seeds[0], (LAYERS, TOKENS, D), 1.0, 6.0, ((0, 2), (1, 256))),
        "train_grad": gaussian(seeds[1], (LAYERS, TOKENS, FF), 1.0, 6.0, ((0, 2), (1, 64), (2, 4))),
        "val_act": gaussian(seeds[2], (LAYERS, VTOK, D), 1.0, 6.0, ((0, 2), (1, 64))),
        "val_grad": gaussian(seeds[3], (LAYERS, VTOK, FF), 1.0, 6.0, ((0, 2), (1, 64), (2, 4))),
    }


def gram_of(left, right):
    return lax.dot_general(left, right, (((1,), (1,)), ((), ())), preferred_element_type=jnp.float32)

def reference(train_act, train_grad, val_act, val_grad):
    running = jnp.zeros((TOKENS,), jnp.float32)
    for layer in range(LAYERS):
        act_gram = gram_of(train_act[layer], val_act[layer])
        grad_gram = gram_of(train_grad[layer], val_grad[layer])
        running = running + lax.optimization_barrier(jnp.sum(act_gram * grad_gram, axis=1))
    return running / math.sqrt(D * FF * VTOK)
```

```python
import math

import jax
import jax.numpy as jnp
from jax import lax
from jax.sharding import Mesh, PartitionSpec as P


CUTS = (0, 7, 14)


def gram_of(left, right):
    return lax.dot_general(
        left, right, (((1,), (1,)), ((), ())), preferred_element_type=jnp.float32
    )


def exchange(blocks, axes):
    return lax.all_to_all(blocks, axes, split_axis=0, concat_axis=0, tiled=True)


def shift(block, axis, by):
    n = lax.axis_size(axis)
    return lax.ppermute(block, axis, [(i, (i + by) % n) for i in range(n)])


def plane(blocks):
    pair, line = lax.axis_size("zl"), lax.axis_size("y")
    shape = blocks.shape[1:]
    blocks = jnp.broadcast_to(blocks[:, None], (pair, line) + shape)
    rows = exchange(blocks.reshape((pair * line,) + shape), ("zl", "y"))
    return rows.reshape(-1, shape[1])


def across(rows):
    moved = [shift(rows, "x", by) for by in (1, -1, 2)]
    return jnp.concatenate([rows, *moved])


def local(train_act, train_grad, val_act, val_grad):
    own, grad, val_a, val_g = train_act[0], train_grad[0], val_act[0], val_grad[0]
    groups, layers, pair = (lax.axis_size(axis) for axis in ("t", "s", "zl"))
    me = lax.axis_index("zl")
    rows, width = own.shape
    hidden = grad.shape[1] * groups
    half = width // pair
    val_total = val_a.shape[0] * lax.axis_size(("x", "zl", "y"))
    factor = 1.0 / math.sqrt(width * hidden * val_total)

    def columns(array, index):
        return lax.dynamic_slice_in_dim(array, index * half, half, 1)

    acts = plane(val_a.reshape(-1, pair, half).transpose(1, 0, 2))
    mine = columns(own, me)
    other = shift(columns(own, 1 - me), "zl", 1)
    unit = grad.shape[1] // CUTS[-1]
    spans = [(unit * a, unit * b) for a, b in zip(CUTS, CUTS[1:])]
    planes = [plane(val_g[None, :, a:b]) for a, b in spans]
    acts = across(acts)
    act_gram = gram_of(jnp.concatenate([mine, other]), acts)
    act_gram = act_gram[:rows] + shift(act_gram[rows:], "zl", 1)
    act_gram = exchange(
        jnp.broadcast_to(act_gram[None], (groups,) + act_gram.shape), "t"
    )
    act_gram = act_gram.reshape(-1, act_gram.shape[-1])

    grad_gram = 0.0
    for i, (a, b) in enumerate(spans):
        grad_gram = lax.optimization_barrier(grad_gram)
        grad_gram = grad_gram + gram_of(grad[:, a:b], across(planes[i]))
    folded = jnp.sum(act_gram * grad_gram, axis=1) * factor
    folded = exchange(folded.reshape(groups * layers, -1), ("t", "s"))
    return jnp.sum(folded, axis=0)


def solution(mesh):
    fine = Mesh(mesh.devices.reshape(4, 2, 8, 4, 2), ("x", "zl", "y", "t", "s"))
    dp = ("x", "zl", "y")
    in_specs = (
        P("s", (*dp, "t"), None),
        P("s", dp, "t"),
        P("s", dp, None),
        P("s", dp, "t"),
    )
    out_specs = P((*dp, "t", "s"))

    return jax.shard_map(local, mesh=fine, in_specs=in_specs, out_specs=out_specs, check_vma=False)
```

```python
import math

import jax
import jax.numpy as jnp
from jax import lax
from jax.sharding import Mesh, PartitionSpec as P


CUTS = (0, 4, 14)


def gram_of(left, right):
    return lax.dot_general(
        left, right, (((1,), (1,)), ((), ())), preferred_element_type=jnp.float32
    )


def exchange(blocks, axes):
    return lax.all_to_all(blocks, axes, split_axis=0, concat_axis=0, tiled=True)


def plane(blocks):
    pair, half = lax.axis_size("zl"), lax.axis_size("yh")
    shape = blocks.shape[2:]
    blocks = jnp.broadcast_to(blocks[:, None], (pair, half, pair) + shape)
    blocks = blocks.reshape((-1,) + shape)
    rows = exchange(blocks, ("zl", "yh", "yl"))
    return rows.reshape(-1, shape[1])


def across(rows):
    n = lax.axis_size("x")
    moved = []
    for by in (1, -1, 2):
        pairs = [(j, (j + by) % n) for j in range(n)]
        moved.append(lax.ppermute(rows, "x", pairs))
    return jnp.concatenate([rows, *moved])


def local(train_act, train_grad, val_act, val_grad):
    own, grad, val_a, val_g = train_act[0], train_grad[0], val_act[0], val_grad[0]
    groups, layers = lax.axis_size("t"), lax.axis_size("s")
    team = ("zl", "yl")
    me, size = lax.axis_index(team), lax.axis_size(team)
    rows, width = own.shape
    hidden = grad.shape[1] * groups
    part = width // size
    val_total = val_a.shape[0] * lax.axis_size(("x", "zl", "yh", "yl"))
    factor = 1.0 / math.sqrt(width * hidden * val_total)
    unit = grad.shape[1] // CUTS[-1]
    spans = [(unit * a, unit * b) for a, b in zip(CUTS, CUTS[1:])]

    first = val_g[:, : spans[0][1]]
    quarters = [val_a[:, q * part : (q + 1) * part] for q in range(size)]
    blocks = jnp.stack([jnp.concatenate([q, first], axis=1) for q in quarters])
    planes = [plane(blocks.reshape((2, 2) + blocks.shape[1:]))]

    pieces = []
    for j in range(size):
        piece = lax.dynamic_slice_in_dim(own, (me ^ j) * part, part, 1)
        if j:
            piece = lax.ppermute(piece, team, [(i, i ^ j) for i in range(size)])
        pieces.append(piece)
    for i, (a, b) in enumerate(spans[1:], 1):
        val = val_g[None, None, :, a:b]
        planes.append(plane(jnp.broadcast_to(val, (2, 2) + val.shape[2:])))

    acts = across(planes[0][:, :part])
    planes[0] = planes[0][:, part:]
    act_gram = gram_of(jnp.concatenate(pieces), acts)
    act_gram = jnp.concatenate(
        [
            lax.dynamic_slice_in_dim(act_gram, (me ^ j) * rows, rows, 0)
            for j in range(size)
        ]
    )
    act_gram = exchange(act_gram.reshape(size, rows, -1), team)
    act_gram = jnp.sum(act_gram, axis=0)
    act_gram = lax.all_gather(act_gram, "t", axis=0, tiled=True)

    grad_gram = 0.0
    for i, (a, b) in enumerate(spans):
        grad_gram = lax.optimization_barrier(grad_gram)
        grad_gram = grad_gram + gram_of(grad[:, a:b], across(planes[i]))
    folded = jnp.sum(act_gram * grad_gram, axis=1) * factor
    folded = exchange(folded.reshape(groups * layers, -1), ("t", "s"))
    return jnp.sum(folded, axis=0)


def solution(mesh):
    axes = ("x", "zl", "yh", "yl", "t", "s")
    fine = Mesh(mesh.devices.reshape(4, 2, 4, 2, 4, 2), axes)
    dp = axes[:4]
    in_specs = (
        P("s", (*dp, "t"), None),
        P("s", dp, "t"),
        P("s", dp, None),
        P("s", dp, "t"),
    )
    out_specs = P((*dp, "t", "s"))

    return jax.shard_map(local, mesh=fine, in_specs=in_specs, out_specs=out_specs, check_vma=False)
```

```python
import math

import jax
import jax.numpy as jnp
from jax import lax
from jax.experimental import pallas as pl
from jax.sharding import Mesh, PartitionSpec as P


CUTS = (0, 7, 28)


def gram_of(left, right):
    return lax.dot_general(
        left, right, (((1,), (1,)), ((), ())), preferred_element_type=jnp.float32
    )


def exchange(blocks, axes):
    return lax.all_to_all(blocks, axes, split_axis=0, concat_axis=0, tiled=True)


def plane(blocks):
    pair, half = lax.axis_size("zl"), lax.axis_size("yh")
    shape = blocks.shape[2:]
    blocks = jnp.broadcast_to(blocks[:, None], (pair, half, pair) + shape)
    blocks = blocks.reshape((-1,) + shape)
    rows = exchange(blocks, ("zl", "yh", "yl"))
    return rows.reshape(-1, shape[1])


def first_blocks(val_a, val_g, part, cols):
    tokens = val_a.shape[0]
    half = lax.axis_size("yh")
    peers = [(z, h, p) for z in range(2) for h in range(half) for p in range(2)]

    def body(a, g, out):
        for i, (z, _, p) in enumerate(peers):
            q = 2 * z + p
            out[i, :, :part] = a[:, q * part : (q + 1) * part]
            out[i, :, part:] = g[...]

    return pl.pallas_call(
        body,
        grid=(1,),
        in_specs=[
            pl.BlockSpec(val_a.shape, lambda i: (0, 0)),
            pl.BlockSpec((tokens, cols), lambda i: (0, 0)),
        ],
        out_specs=pl.BlockSpec((len(peers), tokens, part + cols), lambda i: (0, 0, 0)),
        out_shape=jax.ShapeDtypeStruct((len(peers), tokens, part + cols), val_a.dtype),
        name="first_blocks",
    )(val_a, val_g)


def across(rows):
    n = lax.axis_size("x")
    moved = []
    for by in (2, 1, -1):
        pairs = [(j, (j + by) % n) for j in range(n)]
        moved.append(lax.ppermute(rows, "x", pairs))
    return jnp.concatenate([rows, *moved])


def local(train_act, train_grad, val_act, val_grad):
    own, grad, val_a, val_g = train_act[0], train_grad[0], val_act[0], val_grad[0]
    groups, layers = lax.axis_size("t"), lax.axis_size("s")
    team = ("zl", "yl")
    me, size = lax.axis_index(team), lax.axis_size(team)
    rows, width = own.shape
    hidden = grad.shape[1] * groups
    part = width // size
    val_total = val_a.shape[0] * lax.axis_size(("x", "zl", "yh", "yl"))
    factor = 1.0 / math.sqrt(width * hidden * val_total)
    unit = grad.shape[1] // CUTS[-1]
    spans = [(unit * a, unit * b) for a, b in zip(CUTS, CUTS[1:])]

    blocks = first_blocks(val_a, val_g, part, spans[0][1])
    rows_of = exchange(blocks, ("zl", "yh", "yl"))
    planes = [rows_of.reshape(-1, blocks.shape[2])]

    pieces = []
    for j in range(size):
        piece = lax.dynamic_slice_in_dim(own, (me ^ j) * part, part, 1)
        if j:
            piece = lax.ppermute(piece, team, [(i, i ^ j) for i in range(size)])
        pieces.append(piece)
    for i, (a, b) in enumerate(spans[1:], 1):
        val = val_g[None, None, :, a:b]
        planes.append(plane(jnp.broadcast_to(val, (2, 2) + val.shape[2:])))

    acts = across(planes[0][:, :part])
    planes[0] = planes[0][:, part:]
    act_gram = gram_of(jnp.concatenate(pieces), acts)
    act_gram = jnp.concatenate(
        [
            lax.dynamic_slice_in_dim(act_gram, (me ^ j) * rows, rows, 0)
            for j in range(size)
        ]
    )
    act_gram = exchange(act_gram.reshape(size, rows, -1), team)
    act_gram = jnp.sum(act_gram, axis=0)
    act_gram = jnp.broadcast_to(act_gram[None], (groups,) + act_gram.shape)
    act_gram = exchange(act_gram, "t")
    act_gram = act_gram.reshape(-1, act_gram.shape[-1])

    grad_gram = 0.0
    for i, (a, b) in enumerate(spans):
        grad_gram = lax.optimization_barrier(grad_gram)
        vals = across(planes[i])
        grad_gram = grad_gram + gram_of(grad[:, a:b], vals)
    folded = jnp.sum(act_gram * grad_gram, axis=1) * factor
    folded = exchange(folded.reshape(groups * layers, -1), ("t", "s"))
    return jnp.sum(folded, axis=0)


def solution(mesh):
    axes = ("x", "zl", "yh", "yl", "t", "s")
    fine = Mesh(mesh.devices.reshape(4, 2, 4, 2, 4, 2), axes)
    dp = axes[:4]
    in_specs = (
        P("s", (*dp, "t"), None),
        P("s", dp, "t"),
        P("s", dp, None),
        P("s", dp, "t"),
    )
    out_specs = P((*dp, "t", "s"))

    return jax.shard_map(local, mesh=fine, in_specs=in_specs, out_specs=out_specs, check_vma=False)
```
